256 devices in a mesh: pair: 16 (over x, y), tensor: 16 (over z, core).
Axes of the slice: x: 4, y: 4, z: 8, core: 2. Of those that a mesh axis runs over, the one named last changes fastest.
Arguments:
- queries: bfloat16 [32, 64, 1024], P('pair', 'tensor'), may hold values from -6 to 6
- documents: bfloat16 [64, 128, 1024], P('pair', 'tensor'), may hold values from -6 to 6
- doc_len: int32 [64], replicated, may hold values from 32 to 128
- route: int32 [16, 16], replicated, may hold values from -1 to 3, as said below
- pair_list: int32 [48, 3], P('pair'), may hold values from 0 to 15, as said below
- attn_gain: float32 [1024], replicated
- w_query: bfloat16 [1024, 8192], P(None, 'tensor')
- w_key: bfloat16 [1024, 8192], P(None, 'tensor')
- w_value: bfloat16 [1024, 8192], P(None, 'tensor'), may hold values from -0.1875 to 0.1875
- w_output: bfloat16 [8192, 1024], P('tensor'), may hold values from -0.5 to 0.5
- ffn_gain: float32 [1024], replicated, may hold values from 0.1 to 1.9
- w_in: bfloat16 [1024, 32768], P(None, 'tensor'), may hold values from -0.1875 to 0.1875
- w_down: bfloat16 [32768, 1024], P('tensor'), may hold values from -0.25 to 0.25
Outputs:
- doc_states: bfloat16 [64, 128, 1024], P('pair', 'tensor')
The draws below stay inside these ranges and needn't reach their ends.
Inputs may be any that keep to these rules, and one draw needn't show every extreme that they name: route[s, g] is the local index, among the 4 documents of pair index s, of the one document s sends to owner g, or -1 where it sends none; each owner receives exactly min(6, number of pair indices) documents. `pair_list`: rows p * 3 to p * 3 + 2 belong to owner p; column 0 is below 2; columns 1 and 2 differ and name pair indices that send a document to that owner; each document an owner receives fills one or more roles of its pairs.
All inputs are finite; a program needn't handle non-finite values.
Results may differ from the reference program's by a relative error of at most 0.018.
Values may be sent and summed in bfloat16 or wider, within the bound.
A program may use at most 64 MiB of HBM per device.

```python
import jax
import jax.numpy as jnp
from jax import lax

D = 1024
HEAD = 128
HEADS = 64
FF = 32768
QLEN = 64
DLEN = 128
QUERY_DEV = 2
PAIRS_DEV = 3
DOC_DEV = 4
ROW = 320
NPAIRS = 48
NDOC = 64
NQUERY = 32


def pair_tables(key):
    owners_count = NDOC // DOC_DEV
    needed = min(2 * PAIRS_DEV, owners_count)
    orders = jax.vmap(lambda owner: jax.random.permutation(jax.random.fold_in(key, owner), owners_count))(jnp.arange(owners_count, dtype=jnp.int32))
    sources = orders[:, :needed].astype(jnp.int32)
    picked = jax.random.randint(jax.random.fold_in(key, 1001), (owners_count, needed), 0, DOC_DEV, dtype=jnp.int32)
    targets = jnp.broadcast_to(jnp.arange(owners_count, dtype=jnp.int32)[:, None], (owners_count, needed))
    table = jnp.full((owners_count, owners_count), -1, jnp.int32)
    table = table.at[sources, targets].set(picked)
    role_index = jnp.arange(2 * PAIRS_DEV, dtype=jnp.int32) % needed
    role_sources = sources[:, role_index]
    chosen = jax.random.randint(jax.random.fold_in(key, 1002), (owners_count, PAIRS_DEV), 0, QUERY_DEV, dtype=jnp.int32)
    listing = jnp.stack([chosen, role_sources[:, 0::2], role_sources[:, 1::2]], -1).reshape(owners_count * PAIRS_DEV, 3)
    return (table, listing.astype(jnp.int32))


def draw_route(key, part):
    return pair_tables(jax.random.fold_in(key, 77))[0]


def draw_pair_list(key, part):
    return pair_tables(jax.random.fold_in(key, 77))[1]


def projection_pair(key):
    shape = (D, HEADS * HEAD)
    base = jax.random.normal(jax.random.fold_in(key, 5), shape, jnp.float32) / jnp.sqrt(jnp.float32(D))
    noise = jax.random.normal(jax.random.fold_in(key, 6), shape, jnp.float32) / jnp.sqrt(jnp.float32(D))
    second = noise
    return (base.astype(jnp.bfloat16), second.astype(jnp.bfloat16))


def draw_w_query(key, part):
    return projection_pair(jax.random.fold_in(key, 91))[0]


def draw_w_key(key, part):
    return projection_pair(jax.random.fold_in(key, 91))[1]


def draw_attn_gain(key, part):
    return jax.random.uniform(jax.random.fold_in(key, 3), (D,), jnp.float32, 0.6, 1.4)


def touch_ends(drawn, stream_key, least, largest):
    place = [jax.random.randint(jax.random.fold_in(stream_key, axis), (), 0, length) for axis, length in enumerate(drawn.shape)]
    longest = drawn.shape.index(max(drawn.shape))
    beside = place[:longest] + [(place[longest] + 1) % drawn.shape[longest]] + place[longest + 1:]
    return drawn.at[tuple(place)].set(least).at[tuple(beside)].set(largest)


def block_levels(stream_key, extent, split, low, high):
    def one(axis_at, blocks):
        steps = jax.random.uniform(jax.random.fold_in(jax.random.fold_in(stream_key, 6), axis_at), (blocks,), jnp.float32, low / len(split), high / len(split))
        return jnp.repeat(jnp.exp(steps), extent[axis_at] // blocks).reshape((-1,) + (1,) * (len(extent) - axis_at - 1))

    level = one(*split[0])
    for cut in split[1:]:
        level = level * one(*cut)
    return level


def normal_values(key, shape, width, reach, cuts=(), kind=jnp.bfloat16):
    level = block_levels(key, shape, cuts, -0.22, 0.18) if cuts else 1.0
    values = jax.random.normal(key, shape, jnp.float32) * width * level
    return jnp.minimum(jnp.maximum(values, -reach), reach).astype(kind)


def setup_inputs(seed: int = 0) -> dict:
    arg_keys = jax.random.split(jax.random.key(seed), 14)
    return {
        "queries": normal_values(arg_keys[0], (NQUERY, QLEN, D), 1.0, 6.0, ((0, 16), (1, 16))),
        "documents": normal_values(arg_keys[1], (NDOC, DLEN, D), 1.0, 6.0, ((0, 16), (1, 16))),
        "doc_len": touch_ends(jax.random.randint(arg_keys[2], (NDOC,), DLEN // 4, DLEN + 1), jax.random.fold_in(arg_keys[2], 1), DLEN // 4, DLEN).astype(jnp.int32),
        "route": draw_route(jax.random.fold_in(arg_keys[13], 71), 0),
        "pair_list": draw_pair_list(jax.random.fold_in(arg_keys[13], 71), 0),
        "attn_gain": draw_attn_gain(jax.random.fold_in(arg_keys[13], 71), 0),
        "w_query": draw_w_query(jax.random.fold_in(arg_keys[13], 71), 0),
        "w_key": draw_w_key(jax.random.fold_in(arg_keys[13], 71), 0),
        "w_value": normal_values(arg_keys[8], (D, HEADS * HEAD), D ** -0.5, 0.1875, ((1, 16),)),
        "w_output": normal_values(arg_keys[9], (HEADS * HEAD, D), (HEADS * HEAD // 64) ** -0.5, 0.5, ((0, 16),)),
        "ffn_gain": jnp.clip(1.0 + 0.18 * jax.random.normal(arg_keys[10], (D,), jnp.float32), 0.1, 1.9),
        "w_in": normal_values(arg_keys[11], (D, FF), D ** -0.5, 0.1875, ((1, 16),)),
        "w_down": normal_values(arg_keys[12], (FF, D), (FF // 64) ** -0.5, 0.25, ((0, 16),)),
    }


def rms_norm(values, gain):
    spread = lax.optimization_barrier(jnp.mean(values * values, -1, keepdims=True))
    return values * lax.rsqrt(spread + 1e-06) * gain

def reference(queries, documents, doc_len, route, pair_list, attn_gain, w_query, w_key, w_value, w_output, ffn_gain, w_in, w_down):
    owners = jnp.arange(NPAIRS, dtype=jnp.int32) // PAIRS_DEV
    first_src = pair_list[:, 1].astype(jnp.int32)
    second_src = pair_list[:, 2].astype(jnp.int32)
    first_ids = (first_src * DOC_DEV + route[first_src, owners]).astype(jnp.int32)
    second_ids = (second_src * DOC_DEV + route[second_src, owners]).astype(jnp.int32)
    query_ids = (owners * QUERY_DEV + pair_list[:, 0]).astype(jnp.int32)

    def pair_states(items):
        query_id, first_doc, second_doc = items
        row_tokens = jnp.concatenate([queries[query_id], documents[first_doc], documents[second_doc]], 0)
        position = jnp.arange(ROW, dtype=jnp.int32)
        first_ok = (position >= QLEN) & (position < QLEN + DLEN) & (position - QLEN < doc_len[first_doc])
        second_ok = (position >= QLEN + DLEN) & (position - QLEN - DLEN < doc_len[second_doc])
        key_ok = (position < QLEN) | first_ok | second_ok
        values = row_tokens.astype(jnp.float32)
        normed = rms_norm(values, attn_gain).astype(jnp.bfloat16)
        query_heads = jnp.dot(normed, w_query, preferred_element_type=jnp.float32).astype(jnp.bfloat16).reshape(ROW, HEADS, HEAD)
        key_heads = jnp.dot(normed, w_key, preferred_element_type=jnp.float32).astype(jnp.bfloat16).reshape(ROW, HEADS, HEAD)
        value_heads = jnp.dot(normed, w_value, preferred_element_type=jnp.float32).astype(jnp.bfloat16).reshape(ROW, HEADS, HEAD)
        scores = jnp.einsum('rhd,shd->hrs', query_heads.astype(jnp.float32), key_heads.astype(jnp.float32), precision=lax.Precision.HIGHEST) / jnp.sqrt(jnp.float32(HEAD))
        scores = jnp.where(key_ok[None, None, :], scores, jnp.float32(-1e+30))
        top = lax.optimization_barrier(jnp.max(scores, -1, keepdims=True))
        expo = jnp.exp(scores - top)
        probs = (expo / lax.optimization_barrier(jnp.sum(expo, -1, keepdims=True))).astype(jnp.bfloat16)
        context = jnp.einsum('hrs,shd->rhd', probs.astype(jnp.float32), value_heads.astype(jnp.float32), precision=lax.Precision.HIGHEST)
        context = context.astype(jnp.bfloat16).reshape(ROW, HEADS * HEAD)
        hidden_state = values + jnp.dot(context, w_output, preferred_element_type=jnp.float32)
        ffn_in = rms_norm(hidden_state, ffn_gain).astype(jnp.bfloat16)
        units = jax.nn.relu(jnp.dot(ffn_in, w_in, preferred_element_type=jnp.float32)).astype(jnp.bfloat16)
        layer_out = hidden_state + jnp.dot(units, w_down, preferred_element_type=jnp.float32)
        first_seg = layer_out[QLEN:QLEN + DLEN] * first_ok[QLEN:QLEN + DLEN, None].astype(jnp.float32)
        second_seg = layer_out[QLEN + DLEN:] * second_ok[QLEN + DLEN:, None].astype(jnp.float32)
        return (first_seg, second_seg)
    first_all, second_all = lax.map(pair_states, (query_ids, first_ids, second_ids))
    doc_range = jnp.arange(NDOC, dtype=jnp.int32)
    first_pick = (first_ids[:, None] == doc_range[None, :]).astype(jnp.float32)
    second_pick = (second_ids[:, None] == doc_range[None, :]).astype(jnp.float32)
    totals = jnp.einsum('pn,pld->nld', first_pick, first_all, precision=lax.Precision.HIGHEST)
    totals = totals + jnp.einsum('pn,pld->nld', second_pick, second_all, precision=lax.Precision.HIGHEST)
    return totals.astype(jnp.bfloat16)
```

```python
import functools
import math

import jax
import jax.numpy as jnp
from jax import lax
from jax.experimental import pallas as pl
from jax.experimental.pallas import tpu as pltpu
from jax.sharding import PartitionSpec as P

HEAD = 128
MESH = pl.DeviceIdType.MESH
BF = jnp.bfloat16
F32 = jnp.float32
ORDER = (0, 1, 2, 0, 1, 2, 0, 0, 1, 0, 1, 2, 0, 1, 2, 0, 1, 2, 0, 1, 2, 0, 1, 2, 0, 1, 2, 0, 0, 1, 2, 1, 0, 1, 2, 0, 2, 1, 2, 0, 1, 2, 1, 2, 2)


def dot(a, b):
    return jnp.dot(a, b, preferred_element_type=F32)


def rms_norm(values, gain):
    spread = jnp.mean(values * values, -1, keepdims=True)
    return values * lax.rsqrt(spread + 1e-06) * gain


def layer_kernel(
    owners,
    ring,
    doc_len,
    route,
    pair_list,
    queries,
    documents,
    attn_gain,
    ffn_gain,
    wq_hbm,
    wk_hbm,
    wv_hbm,
    wo_hbm,
    wi_hbm,
    wd_hbm,
    out,
    wq,
    wk,
    wv,
    wo,
    wi,
    wd,
    sent_docs,
    arrived,
    query_blocks,
    gathered,
    tokens,
    q_buf,
    k_buf,
    v_buf,
    context,
    units,
    mine,
    half_out,
    half_in,
    ring_out,
    ring_in,
    ring_sum,
    results,
    back,
    returned,
    weight_sem,
    pair_send,
    pair_recv,
    gather_send,
    gather_recv,
    core_send,
    core_recv,
    ring_send,
    ring_recv,
):
    me = lax.axis_index("pair")
    place = lax.axis_index("tensor")
    z, core = place // 2, place % 2
    way = 1 - 2 * core
    pairs = pair_list.shape[0]
    docs, rows, width = documents.shape
    query_rows = queries.shape[0]
    block = 2 * rows
    half = ring * block
    q_rows = 2 * ring * query_rows
    heads = q_buf.shape[2] // HEAD
    started = []

    def level(k):
        return (z + way * k + 2 * ring) % ring

    def peer(k):
        return (me, level(k) * 2 + core)

    partner = (me, z * 2 + 1 - core)

    def send(src, dst, send_sem, recv_sem, device):
        copy = pltpu.make_async_remote_copy(
            src_ref=src,
            dst_ref=dst,
            send_sem=send_sem,
            recv_sem=recv_sem,
            device_id=device,
            device_id_type=MESH,
        )
        return copy

    def start(copy):
        copy.start()
        started.append(copy)
        return copy

    weights = []
    for n, (source, target) in enumerate(
        ((wk_hbm, wk), (wv_hbm, wv), (wq_hbm, wq), (wo_hbm, wo), (wi_hbm, wi), (wd_hbm, wd))
    ):
        copy = pltpu.make_async_copy(source, target, weight_sem.at[n])
        copy.start()
        weights.append(copy)

    barrier = pltpu.get_barrier_semaphore()
    for d in range(1, owners):
        pl.semaphore_signal(
            barrier, inc=1, device_id=((me + d) % owners, place), device_id_type=MESH
        )
    for device in (peer(1), peer(-1), peer(2), peer(-2), partner):
        pl.semaphore_signal(barrier, inc=1, device_id=device, device_id_type=MESH)

    for o in range(owners):
        sent_docs[o] = documents[jnp.maximum(route[me, o], 0)]
    arrived[me] = sent_docs[me]
    gain = attn_gain[...]
    query_blocks[z] = rms_norm(queries[...].astype(F32), gain).astype(BF)
    pl.semaphore_wait(barrier, owners + 4)

    def pair_copy(d, src, dst, group):
        there = (me + d) % owners
        return send(
            src.at[there],
            dst.at[me],
            pair_send.at[group, d],
            pair_recv.at[group, d],
            (there, place),
        )

    routed = [start(pair_copy(d, sent_docs, arrived, 0)) for d in range(1, owners)]

    def gather_copies(ref_of, slot):
        def one(n, origin, k):
            part = ref_of(level(origin))
            return send(part, part, gather_send.at[slot, n], gather_recv.at[slot, n], peer(k))

        first = [one(0, 0, 2), one(1, 0, -2), one(2, 0, 1), one(3, 0, -1)]
        second = [one(4, -2, 2), one(5, -2, 1), one(6, 2, -1)]
        return first, second

    def query_part(n):
        return query_blocks.at[n]

    query_first, query_second = gather_copies(query_part, 2 * pairs)
    for copy in query_first:
        start(copy)
    query_first[0].wait_recv()
    query_first[1].wait_recv()
    for copy in query_second:
        start(copy)
    for copy in query_first[2:] + query_second:
        copy.wait_recv()
    query_core = start(
        send(
            query_blocks.at[pl.ds(0, ring)],
            query_blocks.at[pl.ds(ring, ring)],
            core_send.at[4 * pairs],
            core_recv.at[4 * pairs],
            partner,
        )
    )
    weights[0].wait()
    weights[1].wait()
    query_core.wait_recv()
    query_tokens = query_blocks[...].astype(F32).reshape(q_rows, width).astype(BF)
    query_keys = dot(query_tokens, wk[...]).astype(BF)
    query_values = dot(query_tokens, wv[...]).astype(BF)
    for p in range(pairs):
        k_buf[p, pl.ds(2 * half, q_rows)] = query_keys
        v_buf[p, pl.ds(2 * half, q_rows)] = query_values
    for copy in routed:
        copy.wait_recv()

    lane = lax.broadcasted_iota(jnp.int32, (1, 2 * half + q_rows), 1)
    local = lax.broadcasted_iota(jnp.int32, (block, 1), 0)

    def pair_row(p):
        chosen = pair_list[p, 0]
        sources = [pair_list[p, 1], pair_list[p, 2]]
        lengths = [doc_len[s * docs + jnp.maximum(route[s, me], 0)] for s in sources]
        own = jnp.concatenate([arrived[s].astype(F32) for s in sources], 0)
        tokens[p] = own

        def gather(stage, values):
            def part(n):
                return gathered.at[stage, p, pl.ds(pl.multiple_of(n * block, block), block)]

            slot = stage * pairs + p
            gathered[stage, p, pl.ds(pl.multiple_of(z * block, block), block)] = values
            first, second = gather_copies(part, slot)
            for copy in first:
                start(copy)
            yield
            first[0].wait_recv()
            first[1].wait_recv()
            for copy in second:
                start(copy)
            yield
            for copy in first[2:] + second:
                copy.wait_recv()
            other = start(
                send(
                    gathered.at[stage, p, pl.ds(0, half)],
                    gathered.at[stage, p, pl.ds(half, half)],
                    core_send.at[slot],
                    core_recv.at[slot],
                    partner,
                )
            )
            yield
            other.wait_recv()

        def core_copy(stage):
            slot = 2 * pairs + stage * pairs + p
            return send(
                half_out.at[stage, p],
                half_in.at[stage, p],
                core_send.at[slot],
                core_recv.at[slot],
                partner,
            )

        def reduce(stage, other):
            slot = stage * pairs + p
            other.wait_recv()
            total = mine[p] + half_in[stage, p].astype(F32)
            mine[p] = total
            ring_out[stage, p] = total.astype(BF)

            def one(n, origin, k, src=None):
                part = (
                    ring_out.at[
                        stage, p, pl.ds(pl.multiple_of(level(origin) * block, block), block)
                    ]
                    if src is None
                    else src
                )
                return start(
                    send(
                        part,
                        ring_in.at[stage, p, n],
                        ring_send.at[slot, n],
                        ring_recv.at[slot, n],
                        peer(k),
                    )
                )

            first = [one(1, 4, 2), one(0, 3, 1), one(2, -3, -1)]
            near = [one(3, 1, 1), one(4, -1, -1)]

            def summand(origin):
                return mine[p, pl.ds(pl.multiple_of(level(origin) * block, block), block)]

            yield
            for copy in first:
                copy.wait_recv()
            ring_sum[stage, p, 0] = (
                summand(2) + ring_in[stage, p, 0].astype(F32) + ring_in[stage, p, 1].astype(F32)
            ).astype(BF)
            ring_sum[stage, p, 1] = (summand(-2) + ring_in[stage, p, 2].astype(F32)).astype(BF)
            far = [
                one(5, 2, 2, ring_sum.at[stage, p, 0]),
                one(6, -2, -2, ring_sum.at[stage, p, 1]),
            ]
            yield
            for copy in near + far:
                copy.wait_recv()
            total = summand(0)
            for n in range(3, 7):
                total = total + ring_in[stage, p, n].astype(F32)
            return total

        yield from gather(0, rms_norm(own, gain).astype(BF))

        if p == 0:
            weights[2].wait()
        x = gathered[0, p]
        q_buf[p] = dot(x, wq[...]).astype(BF)
        k_buf[p, pl.ds(0, 2 * half)] = dot(x, wk[...]).astype(BF)
        v_buf[p, pl.ds(0, 2 * half)] = dot(x, wv[...]).astype(BF)
        yield
        ring_place = (lane % half) // block
        held_by = jnp.where(lane < half, core, 1 - core)
        position = (ring_place * 2 + held_by) * rows + lane % rows
        limit = jnp.where(lane % block < rows, lengths[0], lengths[1])
        doc_ok = jnp.where(position < limit, 1.0, 0.0)
        query_ok = jnp.where((lane % query_rows) // (query_rows // 2) == chosen, 1.0, 0.0)
        key_ok = jnp.where(lane < 2 * half, doc_ok, query_ok)
        for h in range(heads):
            cols = pl.ds(h * HEAD, HEAD)
            scores = lax.dot_general(
                q_buf[p, :, cols],
                k_buf[p, :, cols],
                (((1,), (1,)), ((), ())),
                preferred_element_type=F32,
            ) * (1.0 / math.sqrt(HEAD))
            scores = jnp.where(key_ok > 0.5, scores, -1e30)
            expo = jnp.exp(scores - jnp.max(scores, -1, keepdims=True))
            probs = (expo * (1.0 / jnp.sum(expo, -1, keepdims=True))).astype(BF)
            context[p, :, cols] = dot(probs, v_buf[p, :, cols]).astype(BF)
        if p == 0:
            weights[3].wait()
        half_out[0, p] = dot(context[p, pl.ds(half, half)], wo[...]).astype(BF)
        other = start(core_copy(0))
        mine[p] = dot(context[p, pl.ds(0, half)], wo[...])
        yield
        hidden = tokens[p] + (yield from reduce(0, other))
        tokens[p] = hidden
        yield from gather(1, rms_norm(hidden, ffn_gain[...]).astype(BF))

        if p == 0:
            weights[4].wait()

        def up(n, _):
            cols = pl.ds(pl.multiple_of(n * 512, 512), 512)
            units[:, cols] = jnp.maximum(dot(gathered[1, p], wi[:, cols]), 0.0).astype(BF)
            return 0

        lax.fori_loop(0, units.shape[1] // 512, up, 0)
        yield
        if p == 0:
            weights[5].wait()

        def down(n, _):
            cols = pl.ds(pl.multiple_of(n * 256, 256), 256)
            term = dot(units[...], wd[:, cols])
            mine[p, :, cols] = term[:half]
            half_out[1, p, :, cols] = term[half:].astype(BF)
            return 0

        lax.fori_loop(0, width // 256, down, 0)
        other = start(core_copy(1))
        yield
        layer_out = tokens[p] + (yield from reduce(1, other))
        position = place * rows + local % rows
        limit = jnp.where(local < rows, lengths[0], lengths[1])
        layer_out = jnp.where(position < limit, layer_out, 0.0)
        results[2 * p] = layer_out[:rows].astype(BF)
        results[2 * p + 1] = layer_out[rows:].astype(BF)

    programs = [pair_row(p) for p in range(pairs)]
    for p in ORDER:
        next(programs[p], None)

    results[2 * pairs] = jnp.zeros((rows, width), BF)
    for o in range(owners):
        role = jnp.int32(2 * pairs)
        for p in range(pairs):
            role = jnp.where(pair_list[p, 1] == o, 2 * p, role)
            role = jnp.where(pair_list[p, 2] == o, 2 * p + 1, role)
        back[o] = results[role]
    returned[me] = back[me]
    home = [start(pair_copy(d, back, returned, 1)) for d in range(1, owners)]
    for copy in home:
        copy.wait_recv()
    for k in range(docs):
        total = jnp.zeros((rows, width), F32)
        for o in range(owners):
            total = total + jnp.where(route[me, o] == k, returned[o].astype(F32), 0.0)
        out[k] = total.astype(BF)
    for copy in started:
        copy.wait_send()


def solution(mesh):
    owners = mesh.shape["pair"]
    ring = mesh.shape["tensor"] // 2
    spread = P("pair", "tensor", None)

    def local(
        queries, documents, doc_len, route, pair_list, attn_gain, wq, wk, wv, wo, ffn_gain, wi, wd
    ):
        pairs = pair_list.shape[0]
        docs, rows, width = documents.shape
        query_rows = queries.shape[0] * queries.shape[1]
        head_width, unit_count = wq.shape[1], wi.shape[1]
        block = 2 * rows
        half = ring * block
        keys = 2 * half + 2 * ring * query_rows
        vmem = pl.BlockSpec(memory_space=pltpu.VMEM)
        smem = pl.BlockSpec(memory_space=pltpu.SMEM)
        hbm = pl.BlockSpec(memory_space=pl.ANY)
        dma = pltpu.SemaphoreType.DMA
        return pl.pallas_call(
            functools.partial(layer_kernel, owners, ring),
            out_shape=jax.ShapeDtypeStruct((docs, rows, width), BF),
            in_specs=[smem] * 3 + [vmem] * 4 + [hbm] * 6,
            out_specs=vmem,
            scratch_shapes=[
                pltpu.VMEM(wq.shape, BF),
                pltpu.VMEM(wk.shape, BF),
                pltpu.VMEM(wv.shape, BF),
                pltpu.VMEM(wo.shape, BF),
                pltpu.VMEM(wi.shape, BF),
                pltpu.VMEM(wd.shape, BF),
                pltpu.VMEM((owners, rows, width), BF),
                pltpu.VMEM((owners, rows, width), BF),
                pltpu.VMEM((2 * ring, query_rows, width), BF),
                pltpu.VMEM((2, pairs, 2 * half, width), BF),
                pltpu.VMEM((pairs, block, width), F32),
                pltpu.VMEM((pairs, 2 * half, head_width), BF),
                pltpu.VMEM((pairs, keys, head_width), BF),
                pltpu.VMEM((pairs, keys, head_width), BF),
                pltpu.VMEM((pairs, 2 * half, head_width), BF),
                pltpu.VMEM((2 * half, unit_count), BF),
                pltpu.VMEM((pairs, half, width), F32),
                pltpu.VMEM((2, pairs, half, width), BF),
                pltpu.VMEM((2, pairs, half, width), BF),
                pltpu.VMEM((2, pairs, half, width), BF),
                pltpu.VMEM((2, pairs, 7, block, width), BF),
                pltpu.VMEM((2, pairs, 2, block, width), BF),
                pltpu.VMEM((2 * pairs + 1, rows, width), BF),
                pltpu.VMEM((owners, rows, width), BF),
                pltpu.VMEM((owners, rows, width), BF),
                dma((6,)),
                dma((2, owners)),
                dma((2, owners)),
                dma((2 * pairs + 1, 7)),
                dma((2 * pairs + 1, 7)),
                dma((4 * pairs + 1,)),
                dma((4 * pairs + 1,)),
                dma((2 * pairs, 7)),
                dma((2 * pairs, 7)),
            ],
            compiler_params=pltpu.CompilerParams(
                collective_id=0, has_side_effects=True, vmem_limit_bytes=60 * 1024 * 1024
            ),
        )(
            doc_len,
            route,
            pair_list,
            queries.reshape(query_rows, width),
            documents,
            attn_gain.reshape(1, width),
            ffn_gain.reshape(1, width),
            wq,
            wk,
            wv,
            wo,
            wi,
            wd,
        )

    placed = (
        spread,
        spread,
        P(),
        P(),
        P("pair", None),
        P(),
        P(None, "tensor"),
        P(None, "tensor"),
        P(None, "tensor"),
        P("tensor", None),
        P(),
        P(None, "tensor"),
        P("tensor", None),
    )
    return jax.shard_map(local, mesh=mesh, in_specs=placed, out_specs=spread, check_vma=False)
```

```python
import functools
import math

import jax
import jax.numpy as jnp
from jax import lax
from jax.experimental import pallas as pl
from jax.experimental.pallas import tpu as pltpu
from jax.sharding import PartitionSpec as P

HEAD = 128
MESH = pl.DeviceIdType.MESH
BF = jnp.bfloat16
F32 = jnp.float32
ORDER = (0, 3, 0, 3, 1, 2, 3, 0, 0, 1, 0, 2, 1, 0, 1, 1, 0, 2, 1, 2, 0, 1, 2, 0, 2, 1, 0, 2, 0, 1, 0, 2, 1, 0, 1, 2, 1, 2, 1, 0, 2, 2, 0, 2, 1, 2, 1, 2)


def dot(a, b):
    return jnp.dot(a, b, preferred_element_type=F32)


def rms_norm(values, gain):
    spread = jnp.mean(values * values, -1, keepdims=True)
    return values * lax.rsqrt(spread + 1e-06) * gain


def layer_kernel(
    owners,
    ring,
    doc_len,
    route,
    pair_list,
    queries,
    documents,
    attn_gain,
    ffn_gain,
    wq_hbm,
    wk_hbm,
    wv_hbm,
    wo_hbm,
    wi_hbm,
    wd_hbm,
    out,
    wq,
    wk,
    wv,
    wo,
    wi,
    wd,
    sent_docs,
    arrived,
    query_blocks,
    gathered,
    tokens,
    q_buf,
    k_buf,
    v_buf,
    context,
    units,
    mine,
    half_out,
    half_in,
    ring_out,
    ring_in,
    ring_sum,
    results,
    back,
    returned,
    weight_sem,
    pair_send,
    pair_recv,
    gather_send,
    gather_recv,
    core_send,
    core_recv,
    ring_send,
    ring_recv,
):
    me = lax.axis_index("pair")
    place = lax.axis_index("tensor")
    z, core = place // 2, place % 2
    way = 1 - 2 * core
    pairs = pair_list.shape[0]
    docs, rows, width = documents.shape
    query_count, query_part_rows, _ = queries.shape
    query_rows = query_count * query_part_rows
    block = 2 * rows
    half = ring * block
    q_rows = 2 * ring * query_rows
    heads = q_buf.shape[2] // HEAD
    started = []

    def level(k):
        return (z + way * k + 2 * ring) % ring

    def peer(k):
        return (me, level(k) * 2 + core)

    partner = (me, z * 2 + 1 - core)

    def send(src, dst, send_sem, recv_sem, device):
        copy = pltpu.make_async_remote_copy(
            src_ref=src,
            dst_ref=dst,
            send_sem=send_sem,
            recv_sem=recv_sem,
            device_id=device,
            device_id_type=MESH,
        )
        return copy

    def start(copy):
        copy.start()
        started.append(copy)
        return copy

    barrier = pltpu.get_barrier_semaphore()
    for d in range(1, owners):
        pl.semaphore_signal(
            barrier, inc=1, device_id=((me + d) % owners, place), device_id_type=MESH
        )
    for device in (peer(1), peer(-1), peer(2), peer(-2), partner):
        pl.semaphore_signal(barrier, inc=1, device_id=device, device_id_type=MESH)

    weights = []
    for n, (source, target) in enumerate(
        ((wk_hbm, wk), (wv_hbm, wv), (wq_hbm, wq), (wo_hbm, wo), (wi_hbm, wi), (wd_hbm, wd))
    ):
        copy = pltpu.make_async_copy(source, target, weight_sem.at[n])
        copy.start()
        weights.append(copy)

    for o in range(owners):
        sent_docs[o] = documents[jnp.maximum(route[me, o], 0)]
    arrived[me] = sent_docs[me]
    gain = attn_gain[...]
    own_queries = jnp.concatenate([queries[n].astype(F32) for n in range(query_count)], 0)
    query_blocks[z] = rms_norm(own_queries, gain).astype(BF)
    pl.semaphore_wait(barrier, owners + 4)

    def pair_copy(d, src, dst, group):
        there = (me + d) % owners
        return send(
            src.at[there],
            dst.at[me],
            pair_send.at[group, d],
            pair_recv.at[group, d],
            (there, place),
        )

    routed = [start(pair_copy(d, sent_docs, arrived, 0)) for d in range(1, owners)]

    def gather_copies(ref_of, slot):
        def one(n, origin, k):
            part = ref_of(level(origin))
            return send(part, part, gather_send.at[slot, n], gather_recv.at[slot, n], peer(k))

        first = [one(0, 0, 2), one(1, 0, -2), one(2, 0, 1), one(3, 0, -1)]
        second = [one(4, -2, 2), one(5, -2, 1), one(6, 2, -1)]
        return first, second

    def query_part(n):
        return query_blocks.at[n]

    query_first, query_second = gather_copies(query_part, 2 * pairs)
    for copy in query_first:
        start(copy)
    for copy in routed:
        copy.wait_recv()

    def query_program():
        query_first[0].wait_recv()
        query_first[1].wait_recv()
        for copy in query_second:
            start(copy)
        yield
        for copy in query_first[2:] + query_second:
            copy.wait_recv()
        query_core = start(
            send(
                query_blocks.at[pl.ds(0, ring)],
                query_blocks.at[pl.ds(ring, ring)],
                core_send.at[4 * pairs],
                core_recv.at[4 * pairs],
                partner,
            )
        )
        yield
        weights[0].wait()
        weights[1].wait()
        query_core.wait_recv()
        query_tokens = query_blocks[...].astype(F32).reshape(q_rows, width).astype(BF)
        query_keys = dot(query_tokens, wk[...]).astype(BF)
        query_values = dot(query_tokens, wv[...]).astype(BF)
        for p in range(pairs):
            k_buf[p, pl.ds(2 * half, q_rows)] = query_keys
            v_buf[p, pl.ds(2 * half, q_rows)] = query_values

    lane = lax.broadcasted_iota(jnp.int32, (1, 2 * half + q_rows), 1)
    local = lax.broadcasted_iota(jnp.int32, (block, 1), 0)

    def pair_row(p):
        chosen = pair_list[p, 0]
        sources = [pair_list[p, 1], pair_list[p, 2]]
        lengths = [doc_len[s * docs + jnp.maximum(route[s, me], 0)] for s in sources]
        own = jnp.concatenate([arrived[s].astype(F32) for s in sources], 0)
        tokens[p] = own

        def gather(stage, values):
            def part(n):
                return gathered.at[stage, p, pl.ds(pl.multiple_of(n * block, block), block)]

            slot = stage * pairs + p
            gathered[stage, p, pl.ds(pl.multiple_of(z * block, block), block)] = values
            first, second = gather_copies(part, slot)
            for copy in first:
                start(copy)
            yield
            first[0].wait_recv()
            first[1].wait_recv()
            for copy in second:
                start(copy)
            yield
            for copy in first[2:] + second:
                copy.wait_recv()
            other = start(
                send(
                    gathered.at[stage, p, pl.ds(0, half)],
                    gathered.at[stage, p, pl.ds(half, half)],
                    core_send.at[slot],
                    core_recv.at[slot],
                    partner,
                )
            )
            yield
            other.wait_recv()

        def core_copy(stage):
            slot = 2 * pairs + stage * pairs + p
            return send(
                half_out.at[stage, p],
                half_in.at[stage, p],
                core_send.at[slot],
                core_recv.at[slot],
                partner,
            )

        def reduce(stage, other):
            slot = stage * pairs + p
            other.wait_recv()
            total = mine[p] + half_in[stage, p].astype(F32)
            mine[p] = total
            ring_out[stage, p] = total.astype(BF)

            def one(n, origin, k, src=None):
                part = (
                    ring_out.at[
                        stage, p, pl.ds(pl.multiple_of(level(origin) * block, block), block)
                    ]
                    if src is None
                    else src
                )
                return start(
                    send(
                        part,
                        ring_in.at[stage, p, n],
                        ring_send.at[slot, n],
                        ring_recv.at[slot, n],
                        peer(k),
                    )
                )

            first = [one(1, 4, 2), one(0, 3, 1), one(2, -3, -1)]
            near = [one(3, 1, 1), one(4, -1, -1)]

            def summand(origin):
                return mine[p, pl.ds(pl.multiple_of(level(origin) * block, block), block)]

            yield
            for copy in first:
                copy.wait_recv()
            ring_sum[stage, p, 0] = (
                summand(2) + ring_in[stage, p, 0].astype(F32) + ring_in[stage, p, 1].astype(F32)
            ).astype(BF)
            ring_sum[stage, p, 1] = (summand(-2) + ring_in[stage, p, 2].astype(F32)).astype(BF)
            far = [
                one(5, 2, 2, ring_sum.at[stage, p, 0]),
                one(6, -2, -2, ring_sum.at[stage, p, 1]),
            ]
            yield
            for copy in near + far:
                copy.wait_recv()
            total = summand(0)
            for n in range(3, 7):
                total = total + ring_in[stage, p, n].astype(F32)
            return total

        yield from gather(0, rms_norm(own, gain).astype(BF))

        if p == 0:
            weights[2].wait()
        x = gathered[0, p]
        q_buf[p] = dot(x, wq[...]).astype(BF)
        k_buf[p, pl.ds(0, 2 * half)] = dot(x, wk[...]).astype(BF)
        v_buf[p, pl.ds(0, 2 * half)] = dot(x, wv[...]).astype(BF)
        yield
        ring_place = (lane % half) // block
        held_by = jnp.where(lane < half, core, 1 - core)
        position = (ring_place * 2 + held_by) * rows + lane % rows
        limit = jnp.where(lane % block < rows, lengths[0], lengths[1])
        doc_ok = jnp.where(position < limit, 1.0, 0.0)
        query_ok = jnp.where((lane % query_rows) // query_part_rows == chosen, 1.0, 0.0)
        key_ok = jnp.where(lane < 2 * half, doc_ok, query_ok)
        for h in range(heads):
            cols = pl.ds(h * HEAD, HEAD)
            scores = lax.dot_general(
                q_buf[p, :, cols],
                k_buf[p, :, cols],
                (((1,), (1,)), ((), ())),
                preferred_element_type=F32,
            ) * (1.0 / math.sqrt(HEAD))
            scores = jnp.where(key_ok > 0.5, scores, -1e30)
            expo = jnp.exp(scores - jnp.max(scores, -1, keepdims=True))
            probs = (expo * (1.0 / jnp.sum(expo, -1, keepdims=True))).astype(BF)
            context[p, :, cols] = dot(probs, v_buf[p, :, cols]).astype(BF)
        if p == 0:
            weights[3].wait()
        half_out[0, p] = dot(context[p, pl.ds(half, half)], wo[...]).astype(BF)
        other = start(core_copy(0))
        mine[p] = dot(context[p, pl.ds(0, half)], wo[...])
        yield
        hidden = tokens[p] + (yield from reduce(0, other))
        tokens[p] = hidden
        yield from gather(1, rms_norm(hidden, ffn_gain[...]).astype(BF))

        if p == 0:
            weights[4].wait()

        def up(n, _):
            cols = pl.ds(pl.multiple_of(n * 512, 512), 512)
            units[:, cols] = jnp.maximum(dot(gathered[1, p], wi[:, cols]), 0.0).astype(BF)
            return 0

        lax.fori_loop(0, units.shape[1] // 512, up, 0)
        yield
        if p == 0:
            weights[5].wait()

        def down(n, _):
            cols = pl.ds(pl.multiple_of(n * 256, 256), 256)
            term = dot(units[...], wd[:, cols])
            mine[p, :, cols] = term[:half]
            half_out[1, p, :, cols] = term[half:].astype(BF)
            return 0

        lax.fori_loop(0, width // 256, down, 0)
        other = start(core_copy(1))
        yield
        layer_out = tokens[p] + (yield from reduce(1, other))
        position = place * rows + local % rows
        limit = jnp.where(local < rows, lengths[0], lengths[1])
        layer_out = jnp.where(position < limit, layer_out, 0.0)
        results[2 * p] = layer_out[:rows].astype(BF)
        results[2 * p + 1] = layer_out[rows:].astype(BF)

    programs = [pair_row(p) for p in range(pairs)] + [query_program()]
    for p in ORDER:
        next(programs[p], None)

    results[2 * pairs] = jnp.zeros((rows, width), BF)
    for o in range(owners):
        role = jnp.int32(2 * pairs)
        for p in range(pairs):
            role = jnp.where(pair_list[p, 1] == o, 2 * p, role)
            role = jnp.where(pair_list[p, 2] == o, 2 * p + 1, role)
        back[o] = results[role]
    returned[me] = back[me]
    home = [start(pair_copy(d, back, returned, 1)) for d in range(1, owners)]
    for copy in home:
        copy.wait_recv()
    for k in range(docs):
        total = jnp.zeros((rows, width), F32)
        for o in range(owners):
            total = total + jnp.where(route[me, o] == k, returned[o].astype(F32), 0.0)
        out[k] = total.astype(BF)
    for copy in started:
        copy.wait_send()


def solution(mesh):
    owners = mesh.shape["pair"]
    ring = mesh.shape["tensor"] // 2
    spread = P("pair", "tensor", None)

    def local(
        queries, documents, doc_len, route, pair_list, attn_gain, wq, wk, wv, wo, ffn_gain, wi, wd
    ):
        pairs = pair_list.shape[0]
        docs, rows, width = documents.shape
        query_rows = queries.shape[0] * queries.shape[1]
        head_width, unit_count = wq.shape[1], wi.shape[1]
        block = 2 * rows
        half = ring * block
        keys = 2 * half + 2 * ring * query_rows
        vmem = pl.BlockSpec(memory_space=pltpu.VMEM)
        smem = pl.BlockSpec(memory_space=pltpu.SMEM)
        hbm = pl.BlockSpec(memory_space=pl.ANY)
        dma = pltpu.SemaphoreType.DMA
        return pl.pallas_call(
            functools.partial(layer_kernel, owners, ring),
            out_shape=jax.ShapeDtypeStruct((docs, rows, width), BF),
            in_specs=[smem] * 3 + [vmem] * 4 + [hbm] * 6,
            out_specs=vmem,
            scratch_shapes=[
                pltpu.VMEM(wq.shape, BF),
                pltpu.VMEM(wk.shape, BF),
                pltpu.VMEM(wv.shape, BF),
                pltpu.VMEM(wo.shape, BF),
                pltpu.VMEM(wi.shape, BF),
                pltpu.VMEM(wd.shape, BF),
                pltpu.VMEM((owners, rows, width), BF),
                pltpu.VMEM((owners, rows, width), BF),
                pltpu.VMEM((2 * ring, query_rows, width), BF),
                pltpu.VMEM((2, pairs, 2 * half, width), BF),
                pltpu.VMEM((pairs, block, width), F32),
                pltpu.VMEM((pairs, 2 * half, head_width), BF),
                pltpu.VMEM((pairs, keys, head_width), BF),
                pltpu.VMEM((pairs, keys, head_width), BF),
                pltpu.VMEM((pairs, 2 * half, head_width), BF),
                pltpu.VMEM((2 * half, unit_count), BF),
                pltpu.VMEM((pairs, half, width), F32),
                pltpu.VMEM((2, pairs, half, width), BF),
                pltpu.VMEM((2, pairs, half, width), BF),
                pltpu.VMEM((2, pairs, half, width), BF),
                pltpu.VMEM((2, pairs, 7, block, width), BF),
                pltpu.VMEM((2, pairs, 2, block, width), BF),
                pltpu.VMEM((2 * pairs + 1, rows, width), BF),
                pltpu.VMEM((owners, rows, width), BF),
                pltpu.VMEM((owners, rows, width), BF),
                dma((6,)),
                dma((2, owners)),
                dma((2, owners)),
                dma((2 * pairs + 1, 7)),
                dma((2 * pairs + 1, 7)),
                dma((4 * pairs + 1,)),
                dma((4 * pairs + 1,)),
                dma((2 * pairs, 7)),
                dma((2 * pairs, 7)),
            ],
            compiler_params=pltpu.CompilerParams(
                collective_id=0, has_side_effects=True, vmem_limit_bytes=60 * 1024 * 1024
            ),
        )(
            doc_len,
            route,
            pair_list,
            queries,
            documents,
            attn_gain.reshape(1, width),
            ffn_gain.reshape(1, width),
            wq,
            wk,
            wv,
            wo,
            wi,
            wd,
        )

    placed = (
        spread,
        spread,
        P(),
        P(),
        P("pair", None),
        P(),
        P(None, "tensor"),
        P(None, "tensor"),
        P(None, "tensor"),
        P("tensor", None),
        P(),
        P(None, "tensor"),
        P("tensor", None),
    )
    return jax.shard_map(local, mesh=mesh, in_specs=placed, out_specs=spread, check_vma=False)
```

```python
import functools
import math

import jax
import jax.numpy as jnp
from jax import lax
from jax.experimental import pallas as pl
from jax.experimental.pallas import tpu as pltpu
from jax.sharding import PartitionSpec as P

HEAD = 128
MESH = pl.DeviceIdType.MESH
BF = jnp.bfloat16
F32 = jnp.float32
ORDER = (0, 3, 0, 3, 1, 2, 3, 0, 0, 1, 0, 2, 1, 0, 1, 1, 0, 2, 1, 2, 0, 1, 2, 0, 2, 1, 0, 2, 0, 1, 0, 2, 1, 0, 1, 2, 1, 2, 1, 0, 2, 2, 0, 2, 1, 2, 1, 2)


def dot(a, b):
    return jnp.dot(a, b, preferred_element_type=F32)


def rms_norm(values, gain):
    spread = jnp.mean(values * values, -1, keepdims=True)
    return values * lax.rsqrt(spread + 1e-06) * gain


def layer_kernel(
    owners,
    ring,
    doc_len,
    route,
    pair_list,
    queries,
    documents,
    attn_gain,
    ffn_gain,
    wq_hbm,
    wk_hbm,
    wv_hbm,
    wo_hbm,
    wi_hbm,
    wd_hbm,
    out,
    wq,
    wk,
    wv,
    wo,
    wi,
    wd,
    sent_docs,
    arrived,
    query_blocks,
    gathered,
    tokens,
    q_buf,
    k_buf,
    v_buf,
    context,
    units,
    mine,
    half_out,
    half_in,
    ring_out,
    ring_in,
    ring_sum,
    results,
    back,
    returned,
    weight_sem,
    pair_send,
    pair_recv,
    gather_send,
    gather_recv,
    core_send,
    core_recv,
    ring_send,
    ring_recv,
):
    me = lax.axis_index("pair")
    place = lax.axis_index("tensor")
    z, core = place // 2, place % 2
    way = 1 - 2 * core
    pairs = pair_list.shape[0]
    docs, rows, width = documents.shape
    query_count, query_part_rows, _ = queries.shape
    query_rows = query_count * query_part_rows
    block = 2 * rows
    half = ring * block
    q_rows = 2 * ring * query_rows
    heads = q_buf.shape[2] // HEAD
    started = []

    def level(k):
        return (z + way * k + 2 * ring) % ring

    def peer(k):
        return (me, level(k) * 2 + core)

    partner = (me, z * 2 + 1 - core)

    side = math.isqrt(owners)
    steps = [(a, b) for a in range(side) for b in range(side)]
    steps.sort(key=lambda s: -sum(min(n, side - n) for n in s))

    def owner_at(d):
        a, b = steps[d - 1]
        return (me // side + a) % side * side + (me % side + b) % side

    def send(src, dst, send_sem, recv_sem, device):
        copy = pltpu.make_async_remote_copy(
            src_ref=src,
            dst_ref=dst,
            send_sem=send_sem,
            recv_sem=recv_sem,
            device_id=device,
            device_id_type=MESH,
        )
        return copy

    def start(copy):
        copy.start()
        started.append(copy)
        return copy

    barrier = pltpu.get_barrier_semaphore()
    for d in range(1, owners):
        pl.semaphore_signal(barrier, inc=1, device_id=(owner_at(d), place), device_id_type=MESH)
    for device in (peer(1), peer(-1), peer(2), peer(-2), partner):
        pl.semaphore_signal(barrier, inc=1, device_id=device, device_id_type=MESH)

    weights = []
    for n, (source, target) in enumerate(
        ((wk_hbm, wk), (wv_hbm, wv), (wq_hbm, wq), (wo_hbm, wo), (wi_hbm, wi), (wd_hbm, wd))
    ):
        copy = pltpu.make_async_copy(source, target, weight_sem.at[n])
        copy.start()
        weights.append(copy)

    for o in range(owners):
        sent_docs[o] = documents[jnp.maximum(route[me, o], 0)]
    arrived[me] = sent_docs[me]
    gain = attn_gain[...]
    own_queries = jnp.concatenate([queries[n].astype(F32) for n in range(query_count)], 0)
    query_blocks[z] = rms_norm(own_queries, gain).astype(BF)
    pl.semaphore_wait(barrier, owners + 4)

    def pair_copy(d, src, dst, group):
        there = owner_at(d)
        return send(
            src.at[there],
            dst.at[me],
            pair_send.at[group, d],
            pair_recv.at[group, d],
            (there, place),
        )

    routed = [start(pair_copy(d, sent_docs, arrived, 0)) for d in range(1, owners)]

    def gather_copies(ref_of, slot):
        def one(n, origin, k):
            part = ref_of(level(origin))
            return send(part, part, gather_send.at[slot, n], gather_recv.at[slot, n], peer(k))

        first = [one(0, 0, 2), one(1, 0, -2), one(2, 0, 1), one(3, 0, -1)]
        second = [one(4, -2, 2), one(5, -2, 1), one(6, 2, -1)]
        return first, second

    def query_part(n):
        return query_blocks.at[n]

    query_first, query_second = gather_copies(query_part, 2 * pairs)
    for copy in query_first:
        start(copy)
    results[2 * pairs] = jnp.zeros((rows, width), BF)
    roles = []
    for o in range(owners):
        role = jnp.int32(2 * pairs)
        for p in range(pairs):
            role = jnp.where(pair_list[p, 1] == o, 2 * p, role)
            role = jnp.where(pair_list[p, 2] == o, 2 * p + 1, role)
        roles.append(role)
    for copy in routed:
        copy.wait_recv()

    def query_program():
        query_first[0].wait_recv()
        query_first[1].wait_recv()
        for copy in query_second:
            start(copy)
        yield
        for copy in query_first[2:] + query_second:
            copy.wait_recv()
        query_core = start(
            send(
                query_blocks.at[pl.ds(0, ring)],
                query_blocks.at[pl.ds(ring, ring)],
                core_send.at[4 * pairs],
                core_recv.at[4 * pairs],
                partner,
            )
        )
        yield
        weights[0].wait()
        weights[1].wait()
        query_core.wait_recv()
        query_tokens = query_blocks[...].astype(F32).reshape(q_rows, width).astype(BF)
        query_keys = dot(query_tokens, wk[...]).astype(BF)
        query_values = dot(query_tokens, wv[...]).astype(BF)
        for p in range(pairs):
            k_buf[p, pl.ds(2 * half, q_rows)] = query_keys
            v_buf[p, pl.ds(2 * half, q_rows)] = query_values

    lane = lax.broadcasted_iota(jnp.int32, (1, 2 * half + q_rows), 1)
    local = lax.broadcasted_iota(jnp.int32, (block, 1), 0)

    def pair_row(p):
        chosen = pair_list[p, 0]
        sources = [pair_list[p, 1], pair_list[p, 2]]
        lengths = [doc_len[s * docs + jnp.maximum(route[s, me], 0)] for s in sources]
        own = jnp.concatenate([arrived[s].astype(F32) for s in sources], 0)
        tokens[p] = own

        def gather(stage, values):
            def part(n):
                return gathered.at[stage, p, pl.ds(pl.multiple_of(n * block, block), block)]

            slot = stage * pairs + p
            gathered[stage, p, pl.ds(pl.multiple_of(z * block, block), block)] = values
            first, second = gather_copies(part, slot)
            for copy in first:
                start(copy)
            yield
            first[0].wait_recv()
            first[1].wait_recv()
            for copy in second:
                start(copy)
            yield
            for copy in first[2:] + second:
                copy.wait_recv()
            other = start(
                send(
                    gathered.at[stage, p, pl.ds(0, half)],
                    gathered.at[stage, p, pl.ds(half, half)],
                    core_send.at[slot],
                    core_recv.at[slot],
                    partner,
                )
            )
            yield
            other.wait_recv()

        def core_copy(stage):
            slot = 2 * pairs + stage * pairs + p
            return send(
                half_out.at[stage, p],
                half_in.at[stage, p],
                core_send.at[slot],
                core_recv.at[slot],
                partner,
            )

        def reduce(stage, other):
            slot = stage * pairs + p
            other.wait_recv()
            total = mine[p] + half_in[stage, p].astype(F32)
            mine[p] = total
            ring_out[stage, p] = total.astype(BF)

            def one(n, origin, k, src=None):
                part = (
                    ring_out.at[
                        stage, p, pl.ds(pl.multiple_of(level(origin) * block, block), block)
                    ]
                    if src is None
                    else src
                )
                return start(
                    send(
                        part,
                        ring_in.at[stage, p, n],
                        ring_send.at[slot, n],
                        ring_recv.at[slot, n],
                        peer(k),
                    )
                )

            first = [one(1, 4, 2), one(0, 3, 1), one(2, -3, -1)]
            near = [one(3, 1, 1), one(4, -1, -1)]

            def summand(origin):
                return mine[p, pl.ds(pl.multiple_of(level(origin) * block, block), block)]

            yield
            for copy in first:
                copy.wait_recv()
            ring_sum[stage, p, 0] = (
                summand(2) + ring_in[stage, p, 0].astype(F32) + ring_in[stage, p, 1].astype(F32)
            ).astype(BF)
            ring_sum[stage, p, 1] = (summand(-2) + ring_in[stage, p, 2].astype(F32)).astype(BF)
            far = [
                one(5, 2, 2, ring_sum.at[stage, p, 0]),
                one(6, -2, -2, ring_sum.at[stage, p, 1]),
            ]
            yield
            for copy in near + far:
                copy.wait_recv()
            total = summand(0)
            for n in range(3, 7):
                total = total + ring_in[stage, p, n].astype(F32)
            return total

        yield from gather(0, rms_norm(own, gain).astype(BF))

        if p == 0:
            weights[2].wait()
        x = gathered[0, p]
        q_buf[p] = dot(x, wq[...]).astype(BF)
        k_buf[p, pl.ds(0, 2 * half)] = dot(x, wk[...]).astype(BF)
        v_buf[p, pl.ds(0, 2 * half)] = dot(x, wv[...]).astype(BF)
        yield
        ring_place = (lane % half) // block
        held_by = jnp.where(lane < half, core, 1 - core)
        position = (ring_place * 2 + held_by) * rows + lane % rows
        limit = jnp.where(lane % block < rows, lengths[0], lengths[1])
        doc_ok = jnp.where(position < limit, 1.0, 0.0)
        query_ok = jnp.where((lane % query_rows) // query_part_rows == chosen, 1.0, 0.0)
        key_ok = jnp.where(lane < 2 * half, doc_ok, query_ok)
        for h in range(heads):
            cols = pl.ds(h * HEAD, HEAD)
            scores = lax.dot_general(
                q_buf[p, :, cols],
                k_buf[p, :, cols],
                (((1,), (1,)), ((), ())),
                preferred_element_type=F32,
            ) * (1.0 / math.sqrt(HEAD))
            scores = jnp.where(key_ok > 0.5, scores, -1e30)
            expo = jnp.exp(scores - jnp.max(scores, -1, keepdims=True))
            probs = (expo * (1.0 / jnp.sum(expo, -1, keepdims=True))).astype(BF)
            context[p, :, cols] = dot(probs, v_buf[p, :, cols]).astype(BF)
        if p == 0:
            weights[3].wait()
        half_out[0, p] = dot(context[p, pl.ds(half, half)], wo[...]).astype(BF)
        other = start(core_copy(0))
        mine[p] = dot(context[p, pl.ds(0, half)], wo[...])
        yield
        hidden = tokens[p] + (yield from reduce(0, other))
        tokens[p] = hidden
        yield from gather(1, rms_norm(hidden, ffn_gain[...]).astype(BF))

        if p == 0:
            weights[4].wait()

        def up(n, _):
            cols = pl.ds(pl.multiple_of(n * 512, 512), 512)
            units[:, cols] = jnp.maximum(dot(gathered[1, p], wi[:, cols]), 0.0).astype(BF)
            return 0

        lax.fori_loop(0, units.shape[1] // 512, up, 0)
        yield
        if p == 0:
            weights[5].wait()

        def down(n, _):
            cols = pl.ds(pl.multiple_of(n * 256, 256), 256)
            term = dot(units[...], wd[:, cols])
            mine[p, :, cols] = term[:half]
            half_out[1, p, :, cols] = term[half:].astype(BF)
            return 0

        lax.fori_loop(0, width // 256, down, 0)
        other = start(core_copy(1))
        yield
        layer_out = tokens[p] + (yield from reduce(1, other))
        position = place * rows + local % rows
        limit = jnp.where(local < rows, lengths[0], lengths[1])
        layer_out = jnp.where(position < limit, layer_out, 0.0)
        results[2 * p] = layer_out[:rows].astype(BF)
        results[2 * p + 1] = layer_out[rows:].astype(BF)

    programs = [pair_row(p) for p in range(pairs)] + [query_program()]
    for p in ORDER:
        next(programs[p], None)

    for o in range(owners):
        back[o] = results[roles[o]]
    returned[me] = back[me]
    earlier = len(started)
    home = [start(pair_copy(d, back, returned, 1)) for d in range(1, owners)]
    for copy in started[:earlier]:
        copy.wait_send()
    for copy in home:
        copy.wait_recv()
    for k in range(docs):
        total = jnp.zeros((rows, width), F32)
        for o in range(owners):
            total = total + jnp.where(route[me, o] == k, returned[o].astype(F32), 0.0)
        out[k] = total.astype(BF)
    for copy in home:
        copy.wait_send()


def solution(mesh):
    owners = mesh.shape["pair"]
    ring = mesh.shape["tensor"] // 2
    spread = P("pair", "tensor", None)

    def local(
        queries, documents, doc_len, route, pair_list, attn_gain, wq, wk, wv, wo, ffn_gain, wi, wd
    ):
        pairs = pair_list.shape[0]
        docs, rows, width = documents.shape
        query_rows = queries.shape[0] * queries.shape[1]
        head_width, unit_count = wq.shape[1], wi.shape[1]
        block = 2 * rows
        half = ring * block
        keys = 2 * half + 2 * ring * query_rows
        vmem = pl.BlockSpec(memory_space=pltpu.VMEM)
        smem = pl.BlockSpec(memory_space=pltpu.SMEM)
        hbm = pl.BlockSpec(memory_space=pl.ANY)
        dma = pltpu.SemaphoreType.DMA
        return pl.pallas_call(
            functools.partial(layer_kernel, owners, ring),
            out_shape=jax.ShapeDtypeStruct((docs, rows, width), BF),
            in_specs=[smem] * 3 + [vmem] * 4 + [hbm] * 6,
            out_specs=vmem,
            scratch_shapes=[
                pltpu.VMEM(wq.shape, BF),
                pltpu.VMEM(wk.shape, BF),
                pltpu.VMEM(wv.shape, BF),
                pltpu.VMEM(wo.shape, BF),
                pltpu.VMEM(wi.shape, BF),
                pltpu.VMEM(wd.shape, BF),
                pltpu.VMEM((owners, rows, width), BF),
                pltpu.VMEM((owners, rows, width), BF),
                pltpu.VMEM((2 * ring, query_rows, width), BF),
                pltpu.VMEM((2, pairs, 2 * half, width), BF),
                pltpu.VMEM((pairs, block, width), F32),
                pltpu.VMEM((pairs, 2 * half, head_width), BF),
                pltpu.VMEM((pairs, keys, head_width), BF),
                pltpu.VMEM((pairs, keys, head_width), BF),
                pltpu.VMEM((pairs, 2 * half, head_width), BF),
                pltpu.VMEM((2 * half, unit_count), BF),
                pltpu.VMEM((pairs, half, width), F32),
                pltpu.VMEM((2, pairs, half, width), BF),
                pltpu.VMEM((2, pairs, half, width), BF),
                pltpu.VMEM((2, pairs, half, width), BF),
                pltpu.VMEM((2, pairs, 7, block, width), BF),
                pltpu.VMEM((2, pairs, 2, block, width), BF),
                pltpu.VMEM((2 * pairs + 1, rows, width), BF),
                pltpu.VMEM((owners, rows, width), BF),
                pltpu.VMEM((owners, rows, width), BF),
                dma((6,)),
                dma((2, owners)),
                dma((2, owners)),
                dma((2 * pairs + 1, 7)),
                dma((2 * pairs + 1, 7)),
                dma((4 * pairs + 1,)),
                dma((4 * pairs + 1,)),
                dma((2 * pairs, 7)),
                dma((2 * pairs, 7)),
            ],
            compiler_params=pltpu.CompilerParams(
                collective_id=0, has_side_effects=True, vmem_limit_bytes=60 * 1024 * 1024
            ),
        )(
            doc_len,
            route,
            pair_list,
            queries,
            documents,
            attn_gain.reshape(1, width),
            ffn_gain.reshape(1, width),
            wq,
            wk,
            wv,
            wo,
            wi,
            wd,
        )

    placed = (
        spread,
        spread,
        P(),
        P(),
        P("pair", None),
        P(),
        P(None, "tensor"),
        P(None, "tensor"),
        P(None, "tensor"),
        P("tensor", None),
        P(),
        P(None, "tensor"),
        P("tensor", None),
    )
    return jax.shard_map(local, mesh=mesh, in_specs=placed, out_specs=spread, check_vma=False)
```

```python
import functools
import math

import jax
import jax.numpy as jnp
from jax import lax
from jax.experimental import pallas as pl
from jax.experimental.pallas import tpu as pltpu
from jax.sharding import PartitionSpec as P

HEAD = 128
MESH = pl.DeviceIdType.MESH
BF = jnp.bfloat16
F32 = jnp.float32
ORDER = (0, 3, 0, 3, 1, 2, 3, 0, 0, 1, 0, 2, 1, 0, 1, 1, 0, 2, 1, 2, 0, 1, 2, 0, 2, 1, 0, 2, 0, 1, 0, 2, 1, 0, 1, 2, 1, 2, 1, 0, 2, 2, 0, 2, 1, 2, 1, 2)


def dot(a, b):
    return jnp.dot(a, b, preferred_element_type=F32)


def rms_norm(values, gain):
    spread = jnp.mean(values * values, -1, keepdims=True)
    return values * lax.rsqrt(spread + 1e-06) * gain


def layer_kernel(
    owners,
    ring,
    doc_len_hbm,
    route_hbm,
    pair_list_hbm,
    queries_hbm,
    documents_hbm,
    attn_gain_hbm,
    ffn_gain_hbm,
    wq_hbm,
    wk_hbm,
    wv_hbm,
    wo_hbm,
    wi_hbm,
    wd_hbm,
    out,
    doc_len,
    route,
    pair_list,
    queries,
    documents,
    attn_gain,
    ffn_gain,
    wq,
    wk,
    wv,
    wo,
    wi,
    wd,
    sent_docs,
    arrived,
    query_blocks,
    gathered,
    tokens,
    q_buf,
    k_buf,
    v_buf,
    context,
    units,
    mine,
    half_out,
    half_in,
    ring_out,
    ring_in,
    ring_sum,
    results,
    back,
    returned,
    input_sem,
    weight_sem,
    pair_send,
    pair_recv,
    gather_send,
    gather_recv,
    core_send,
    core_recv,
    ring_send,
    ring_recv,
):
    me = lax.axis_index("pair")
    place = lax.axis_index("tensor")
    z, core = place // 2, place % 2
    way = 1 - 2 * core
    pairs = pair_list.shape[0]
    docs, rows, width = documents.shape
    query_count, query_part_rows, _ = queries.shape
    query_rows = query_count * query_part_rows
    block = 2 * rows
    half = ring * block
    q_rows = 2 * ring * query_rows
    heads = q_buf.shape[2] // HEAD
    started = []

    def level(k):
        return (z + way * k + 2 * ring) % ring

    def peer(k):
        return (me, level(k) * 2 + core)

    partner = (me, z * 2 + 1 - core)

    side = math.isqrt(owners)
    steps = [(a, b) for a in range(side) for b in range(side)]
    steps.sort(key=lambda s: -sum(min(n, side - n) for n in s))

    def owner_at(d):
        a, b = steps[d - 1]
        return (me // side + a) % side * side + (me % side + b) % side

    def send(src, dst, send_sem, recv_sem, device):
        copy = pltpu.make_async_remote_copy(
            src_ref=src,
            dst_ref=dst,
            send_sem=send_sem,
            recv_sem=recv_sem,
            device_id=device,
            device_id_type=MESH,
        )
        return copy

    def start(copy):
        copy.start()
        started.append(copy)
        return copy

    barrier = pltpu.get_barrier_semaphore()
    for d in range(1, owners):
        pl.semaphore_signal(barrier, inc=1, device_id=(owner_at(d), place), device_id_type=MESH)
    for device in (peer(1), peer(-1), peer(2), peer(-2), partner):
        pl.semaphore_signal(barrier, inc=1, device_id=device, device_id_type=MESH)

    inputs = []
    for n, (source, target) in enumerate(
        (
            (route_hbm, route),
            (documents_hbm, documents),
            (queries_hbm, queries),
            (attn_gain_hbm, attn_gain),
            (pair_list_hbm, pair_list),
            (doc_len_hbm, doc_len),
            (ffn_gain_hbm, ffn_gain),
        )
    ):
        copy = pltpu.make_async_copy(source, target, input_sem.at[n])
        copy.start()
        inputs.append(copy)
    weights = []
    for n, (source, target) in enumerate(
        ((wk_hbm, wk), (wv_hbm, wv), (wq_hbm, wq), (wo_hbm, wo), (wi_hbm, wi), (wd_hbm, wd))
    ):
        copy = pltpu.make_async_copy(source, target, weight_sem.at[n])
        copy.start()
        weights.append(copy)

    for copy in inputs:
        copy.wait()
    for o in range(owners):
        sent_docs[o] = documents[jnp.maximum(route[me, o], 0)]
    arrived[me] = sent_docs[me]
    gain = attn_gain[...]
    own_queries = jnp.concatenate([queries[n].astype(F32) for n in range(query_count)], 0)
    query_blocks[z] = rms_norm(own_queries, gain).astype(BF)
    pl.semaphore_wait(barrier, owners + 4)

    def pair_copy(d, src, dst, group):
        there = owner_at(d)
        return send(
            src.at[there],
            dst.at[me],
            pair_send.at[group, d],
            pair_recv.at[group, d],
            (there, place),
        )

    routed = [start(pair_copy(d, sent_docs, arrived, 0)) for d in range(1, owners)]

    def gather_copies(ref_of, slot):
        def one(n, origin, k):
            part = ref_of(level(origin))
            return send(part, part, gather_send.at[slot, n], gather_recv.at[slot, n], peer(k))

        first = [one(0, 0, 2), one(1, 0, -2), one(2, 0, 1), one(3, 0, -1)]
        second = [one(4, -2, 2), one(5, -2, 1), one(6, 2, -1)]
        return first, second

    def query_part(n):
        return query_blocks.at[n]

    query_first, query_second = gather_copies(query_part, 2 * pairs)
    for copy in query_first:
        start(copy)
    results[2 * pairs] = jnp.zeros((rows, width), BF)
    roles = []
    for o in range(owners):
        role = jnp.int32(2 * pairs)
        for p in range(pairs):
            role = jnp.where(pair_list[p, 1] == o, 2 * p, role)
            role = jnp.where(pair_list[p, 2] == o, 2 * p + 1, role)
        roles.append(role)
    for copy in routed:
        copy.wait_recv()

    def query_program():
        query_first[0].wait_recv()
        query_first[1].wait_recv()
        for copy in query_second:
            start(copy)
        yield
        for copy in query_first[2:] + query_second:
            copy.wait_recv()
        query_core = start(
            send(
                query_blocks.at[pl.ds(0, ring)],
                query_blocks.at[pl.ds(ring, ring)],
                core_send.at[4 * pairs],
                core_recv.at[4 * pairs],
                partner,
            )
        )
        yield
        weights[0].wait()
        weights[1].wait()
        query_core.wait_recv()
        query_tokens = query_blocks[...].astype(F32).reshape(q_rows, width).astype(BF)
        query_keys = dot(query_tokens, wk[...]).astype(BF)
        query_values = dot(query_tokens, wv[...]).astype(BF)
        for p in range(pairs):
            k_buf[p, pl.ds(2 * half, q_rows)] = query_keys
            v_buf[p, pl.ds(2 * half, q_rows)] = query_values

    lane = lax.broadcasted_iota(jnp.int32, (1, 2 * half + q_rows), 1)
    local = lax.broadcasted_iota(jnp.int32, (block, 1), 0)

    def pair_row(p):
        chosen = pair_list[p, 0]
        sources = [pair_list[p, 1], pair_list[p, 2]]
        lengths = [doc_len[s * docs + jnp.maximum(route[s, me], 0)] for s in sources]
        own = jnp.concatenate([arrived[s].astype(F32) for s in sources], 0)
        tokens[p] = own

        def gather(stage, values):
            def part(n):
                return gathered.at[stage, p, pl.ds(pl.multiple_of(n * block, block), block)]

            slot = stage * pairs + p
            gathered[stage, p, pl.ds(pl.multiple_of(z * block, block), block)] = values
            first, second = gather_copies(part, slot)
            for copy in first:
                start(copy)
            yield
            first[0].wait_recv()
            first[1].wait_recv()
            for copy in second:
                start(copy)
            yield
            for copy in first[2:] + second:
                copy.wait_recv()
            other = start(
                send(
                    gathered.at[stage, p, pl.ds(0, half)],
                    gathered.at[stage, p, pl.ds(half, half)],
                    core_send.at[slot],
                    core_recv.at[slot],
                    partner,
                )
            )
            yield
            other.wait_recv()

        def core_copy(stage):
            slot = 2 * pairs + stage * pairs + p
            return send(
                half_out.at[stage, p],
                half_in.at[stage, p],
                core_send.at[slot],
                core_recv.at[slot],
                partner,
            )

        def reduce(stage, other):
            slot = stage * pairs + p
            other.wait_recv()
            total = mine[p] + half_in[stage, p].astype(F32)
            mine[p] = total
            ring_out[stage, p] = total.astype(BF)

            def one(n, origin, k, src=None):
                part = (
                    ring_out.at[
                        stage, p, pl.ds(pl.multiple_of(level(origin) * block, block), block)
                    ]
                    if src is None
                    else src
                )
                return start(
                    send(
                        part,
                        ring_in.at[stage, p, n],
                        ring_send.at[slot, n],
                        ring_recv.at[slot, n],
                        peer(k),
                    )
                )

            first = [one(1, 4, 2), one(0, 3, 1), one(2, -3, -1)]
            near = [one(3, 1, 1), one(4, -1, -1)]

            def summand(origin):
                return mine[p, pl.ds(pl.multiple_of(level(origin) * block, block), block)]

            yield
            for copy in first:
                copy.wait_recv()
            ring_sum[stage, p, 0] = (
                summand(2) + ring_in[stage, p, 0].astype(F32) + ring_in[stage, p, 1].astype(F32)
            ).astype(BF)
            ring_sum[stage, p, 1] = (summand(-2) + ring_in[stage, p, 2].astype(F32)).astype(BF)
            far = [
                one(5, 2, 2, ring_sum.at[stage, p, 0]),
                one(6, -2, -2, ring_sum.at[stage, p, 1]),
            ]
            yield
            for copy in near + far:
                copy.wait_recv()
            total = summand(0)
            for n in range(3, 7):
                total = total + ring_in[stage, p, n].astype(F32)
            return total

        yield from gather(0, rms_norm(own, gain).astype(BF))

        if p == 0:
            weights[2].wait()
        x = gathered[0, p]
        q_buf[p] = dot(x, wq[...]).astype(BF)
        k_buf[p, pl.ds(0, 2 * half)] = dot(x, wk[...]).astype(BF)
        v_buf[p, pl.ds(0, 2 * half)] = dot(x, wv[...]).astype(BF)
        yield
        ring_place = (lane % half) // block
        held_by = jnp.where(lane < half, core, 1 - core)
        position = (ring_place * 2 + held_by) * rows + lane % rows
        limit = jnp.where(lane % block < rows, lengths[0], lengths[1])
        doc_ok = jnp.where(position < limit, 1.0, 0.0)
        query_ok = jnp.where((lane % query_rows) // query_part_rows == chosen, 1.0, 0.0)
        key_ok = jnp.where(lane < 2 * half, doc_ok, query_ok)
        for h in range(heads):
            cols = pl.ds(h * HEAD, HEAD)
            scores = lax.dot_general(
                q_buf[p, :, cols],
                k_buf[p, :, cols],
                (((1,), (1,)), ((), ())),
                preferred_element_type=F32,
            ) * (1.0 / math.sqrt(HEAD))
            scores = jnp.where(key_ok > 0.5, scores, -1e30)
            expo = jnp.exp(scores - jnp.max(scores, -1, keepdims=True))
            probs = (expo * (1.0 / jnp.sum(expo, -1, keepdims=True))).astype(BF)
            context[p, :, cols] = dot(probs, v_buf[p, :, cols]).astype(BF)
        if p == 0:
            weights[3].wait()
        half_out[0, p] = dot(context[p, pl.ds(half, half)], wo[...]).astype(BF)
        other = start(core_copy(0))
        mine[p] = dot(context[p, pl.ds(0, half)], wo[...])
        yield
        hidden = tokens[p] + (yield from reduce(0, other))
        tokens[p] = hidden
        yield from gather(1, rms_norm(hidden, ffn_gain[...]).astype(BF))

        if p == 0:
            weights[4].wait()

        def up(n, _):
            cols = pl.ds(pl.multiple_of(n * 512, 512), 512)
            units[:, cols] = jnp.maximum(dot(gathered[1, p], wi[:, cols]), 0.0).astype(BF)
            return 0

        lax.fori_loop(0, units.shape[1] // 512, up, 0)
        yield
        if p == 0:
            weights[5].wait()

        def down(n, _):
            cols = pl.ds(pl.multiple_of(n * 256, 256), 256)
            term = dot(units[...], wd[:, cols])
            mine[p, :, cols] = term[:half]
            half_out[1, p, :, cols] = term[half:].astype(BF)
            return 0

        lax.fori_loop(0, width // 256, down, 0)
        other = start(core_copy(1))
        yield
        layer_out = tokens[p] + (yield from reduce(1, other))
        position = place * rows + local % rows
        limit = jnp.where(local < rows, lengths[0], lengths[1])
        layer_out = jnp.where(position < limit, layer_out, 0.0)
        results[2 * p] = layer_out[:rows].astype(BF)
        results[2 * p + 1] = layer_out[rows:].astype(BF)

    programs = [pair_row(p) for p in range(pairs)] + [query_program()]
    for p in ORDER:
        next(programs[p], None)

    for o in range(owners):
        back[o] = results[roles[o]]
    returned[me] = back[me]
    earlier = len(started)
    home = [start(pair_copy(d, back, returned, 1)) for d in range(1, owners)]
    for copy in started[:earlier]:
        copy.wait_send()
    for copy in home:
        copy.wait_recv()
    for k in range(docs):
        total = jnp.zeros((rows, width), F32)
        for o in range(owners):
            total = total + jnp.where(route[me, o] == k, returned[o].astype(F32), 0.0)
        out[k] = total.astype(BF)
    for copy in home:
        copy.wait_send()


def solution(mesh):
    owners = mesh.shape["pair"]
    ring = mesh.shape["tensor"] // 2
    spread = P("pair", "tensor", None)

    def local(
        queries, documents, doc_len, route, pair_list, attn_gain, wq, wk, wv, wo, ffn_gain, wi, wd
    ):
        pairs = pair_list.shape[0]
        docs, rows, width = documents.shape
        query_rows = queries.shape[0] * queries.shape[1]
        head_width, unit_count = wq.shape[1], wi.shape[1]
        block = 2 * rows
        half = ring * block
        keys = 2 * half + 2 * ring * query_rows
        vmem = pl.BlockSpec(memory_space=pltpu.VMEM)
        hbm = pl.BlockSpec(memory_space=pl.ANY)
        dma = pltpu.SemaphoreType.DMA
        return pl.pallas_call(
            functools.partial(layer_kernel, owners, ring),
            out_shape=pltpu.VMEM((docs, rows, width), BF),
            in_specs=[hbm] * 13,
            out_specs=vmem,
            scratch_shapes=[
                pltpu.SMEM(doc_len.shape, jnp.int32),
                pltpu.SMEM(route.shape, jnp.int32),
                pltpu.SMEM(pair_list.shape, jnp.int32),
                pltpu.VMEM(queries.shape, BF),
                pltpu.VMEM(documents.shape, BF),
                pltpu.VMEM((1, width), F32),
                pltpu.VMEM((1, width), F32),
                pltpu.VMEM(wq.shape, BF),
                pltpu.VMEM(wk.shape, BF),
                pltpu.VMEM(wv.shape, BF),
                pltpu.VMEM(wo.shape, BF),
                pltpu.VMEM(wi.shape, BF),
                pltpu.VMEM(wd.shape, BF),
                pltpu.VMEM((owners, rows, width), BF),
                pltpu.VMEM((owners, rows, width), BF),
                pltpu.VMEM((2 * ring, query_rows, width), BF),
                pltpu.VMEM((2, pairs, 2 * half, width), BF),
                pltpu.VMEM((pairs, block, width), F32),
                pltpu.VMEM((pairs, 2 * half, head_width), BF),
                pltpu.VMEM((pairs, keys, head_width), BF),
                pltpu.VMEM((pairs, keys, head_width), BF),
                pltpu.VMEM((pairs, 2 * half, head_width), BF),
                pltpu.VMEM((2 * half, unit_count), BF),
                pltpu.VMEM((pairs, half, width), F32),
                pltpu.VMEM((2, pairs, half, width), BF),
                pltpu.VMEM((2, pairs, half, width), BF),
                pltpu.VMEM((2, pairs, half, width), BF),
                pltpu.VMEM((2, pairs, 7, block, width), BF),
                pltpu.VMEM((2, pairs, 2, block, width), BF),
                pltpu.VMEM((2 * pairs + 1, rows, width), BF),
                pltpu.VMEM((owners, rows, width), BF),
                pltpu.VMEM((owners, rows, width), BF),
                dma((7,)),
                dma((6,)),
                dma((2, owners)),
                dma((2, owners)),
                dma((2 * pairs + 1, 7)),
                dma((2 * pairs + 1, 7)),
                dma((4 * pairs + 1,)),
                dma((4 * pairs + 1,)),
                dma((2 * pairs, 7)),
                dma((2 * pairs, 7)),
            ],
            compiler_params=pltpu.CompilerParams(
                collective_id=0, has_side_effects=True, vmem_limit_bytes=60 * 1024 * 1024
            ),
        )(
            doc_len,
            route,
            pair_list,
            queries,
            documents,
            attn_gain.reshape(1, width),
            ffn_gain.reshape(1, width),
            wq,
            wk,
            wv,
            wo,
            wi,
            wd,
        )

    placed = (
        spread,
        spread,
        P(),
        P(),
        P("pair", None),
        P(),
        P(None, "tensor"),
        P(None, "tensor"),
        P(None, "tensor"),
        P("tensor", None),
        P(),
        P(None, "tensor"),
        P("tensor", None),
    )
    return jax.shard_map(local, mesh=mesh, in_specs=placed, out_specs=spread, check_vma=False)
```

```python
import functools
import math

import jax
import jax.numpy as jnp
from jax import lax
from jax.experimental import pallas as pl
from jax.experimental.pallas import tpu as pltpu
from jax.sharding import PartitionSpec as P

HEAD = 128
MESH = pl.DeviceIdType.MESH
BF = jnp.bfloat16
F32 = jnp.float32
ORDER = (0, 3, 0, 3, 1, 2, 3, 0, 0, 1, 0, 2, 1, 0, 1, 1, 0, 2, 1, 2, 0, 1, 2, 0, 2, 1, 0, 2, 0, 1, 0, 2, 1, 0, 1, 2, 1, 2, 1, 0, 2, 2, 0, 2, 1, 2, 1, 2)


def dot(a, b):
    return jnp.dot(a, b, preferred_element_type=F32)


def rms_norm(values, gain):
    spread = jnp.mean(values * values, -1, keepdims=True)
    return values * lax.rsqrt(spread + 1e-06) * gain


def layer_kernel(
    owners,
    ring,
    doc_len_hbm,
    route_hbm,
    pair_list_hbm,
    queries_hbm,
    documents_hbm,
    attn_gain_hbm,
    ffn_gain_hbm,
    wq_hbm,
    wk_hbm,
    wv_hbm,
    wo_hbm,
    wi_hbm,
    wd_hbm,
    out,
    doc_len,
    route,
    pair_list,
    queries,
    documents,
    attn_gain,
    ffn_gain,
    wq,
    wk,
    wv,
    wo,
    wi,
    wd,
    sent_docs,
    arrived,
    query_blocks,
    gathered,
    tokens,
    q_buf,
    k_buf,
    v_buf,
    context,
    units,
    mine,
    half_out,
    half_in,
    ring_out,
    ring_in,
    ring_sum,
    results,
    back,
    returned,
    input_sem,
    weight_sem,
    pair_send,
    pair_recv,
    gather_send,
    gather_recv,
    core_send,
    core_recv,
    ring_send,
    ring_recv,
):
    me = lax.axis_index("pair")
    place = lax.axis_index("tensor")
    z, core = place // 2, place % 2
    way = 1 - 2 * core
    pairs = pair_list.shape[0]
    docs, rows, width = documents.shape
    query_count, query_part_rows, _ = queries.shape
    query_rows = query_count * query_part_rows
    block = 2 * rows
    half = ring * block
    q_rows = 2 * ring * query_rows
    heads = q_buf.shape[2] // HEAD
    started = []

    def level(k):
        return (z + way * k + 2 * ring) % ring

    def peer(k):
        return (me, level(k) * 2 + core)

    partner = (me, z * 2 + 1 - core)

    side = math.isqrt(owners)
    steps = [(a, b) for a in range(side) for b in range(side)]
    steps.sort(key=lambda s: -sum(min(n, side - n) for n in s))

    def owner_at(d):
        a, b = steps[d - 1]
        return (me // side + a) % side * side + (me % side + b) % side

    def send(src, dst, send_sem, recv_sem, device):
        copy = pltpu.make_async_remote_copy(
            src_ref=src,
            dst_ref=dst,
            send_sem=send_sem,
            recv_sem=recv_sem,
            device_id=device,
            device_id_type=MESH,
        )
        return copy

    def start(copy):
        copy.start()
        started.append(copy)
        return copy

    barrier = pltpu.get_barrier_semaphore()
    for d in range(1, owners):
        pl.semaphore_signal(barrier, inc=1, device_id=(owner_at(d), place), device_id_type=MESH)
    for device in (peer(1), peer(-1), peer(2), peer(-2), partner):
        pl.semaphore_signal(barrier, inc=1, device_id=device, device_id_type=MESH)

    inputs = []
    for n, (source, target) in enumerate(
        (
            (route_hbm, route),
            (documents_hbm, documents),
            (queries_hbm, queries),
            (attn_gain_hbm, attn_gain),
            (pair_list_hbm, pair_list),
            (doc_len_hbm, doc_len),
            (ffn_gain_hbm, ffn_gain),
        )
    ):
        copy = pltpu.make_async_copy(source, target, input_sem.at[n])
        copy.start()
        inputs.append(copy)
    weights = []
    for n, (source, target) in enumerate(
        ((wk_hbm, wk), (wv_hbm, wv), (wq_hbm, wq), (wo_hbm, wo), (wi_hbm, wi), (wd_hbm, wd))
    ):
        copy = pltpu.make_async_copy(source, target, weight_sem.at[n])
        copy.start()
        weights.append(copy)

    for copy in inputs:
        copy.wait()
    for o in range(owners):
        sent_docs[o] = documents[jnp.maximum(route[me, o], 0)]
    arrived[me] = sent_docs[me]
    gain = attn_gain[...]
    own_queries = jnp.concatenate([queries[n].astype(F32) for n in range(query_count)], 0)
    query_blocks[z] = rms_norm(own_queries, gain).astype(BF)
    pl.semaphore_wait(barrier, owners + 4)

    def pair_copy(d, src, dst, group):
        there = owner_at(d)
        return send(
            src.at[there],
            dst.at[me],
            pair_send.at[group, d],
            pair_recv.at[group, d],
            (there, place),
        )

    routed = [start(pair_copy(d, sent_docs, arrived, 0)) for d in range(1, owners)]

    def gather_copies(ref_of, slot):
        def one(n, origin, k):
            part = ref_of(level(origin))
            return send(part, part, gather_send.at[slot, n], gather_recv.at[slot, n], peer(k))

        first = [one(0, 0, 2), one(1, 0, -2), one(2, 0, 1), one(3, 0, -1)]
        second = [one(4, -2, 2), one(5, -2, 1), one(6, 2, -1)]
        return first, second

    def query_part(n):
        return query_blocks.at[n]

    query_first, query_second = gather_copies(query_part, 2 * pairs)
    for copy in query_first:
        start(copy)
    results[2 * pairs] = jnp.zeros((rows, width), BF)
    roles = []
    for o in range(owners):
        role = jnp.int32(2 * pairs)
        for p in range(pairs):
            role = jnp.where(pair_list[p, 1] == o, 2 * p, role)
            role = jnp.where(pair_list[p, 2] == o, 2 * p + 1, role)
        roles.append(role)
    for copy in routed:
        copy.wait_recv()

    def query_program():
        query_first[0].wait_recv()
        query_first[1].wait_recv()
        for copy in query_second:
            start(copy)
        yield
        for copy in query_first[2:] + query_second:
            copy.wait_recv()
        query_core = start(
            send(
                query_blocks.at[pl.ds(0, ring)],
                query_blocks.at[pl.ds(ring, ring)],
                core_send.at[4 * pairs],
                core_recv.at[4 * pairs],
                partner,
            )
        )
        yield
        weights[0].wait()
        weights[1].wait()
        query_core.wait_recv()
        query_tokens = query_blocks[...].astype(F32).reshape(q_rows, width).astype(BF)
        query_keys = dot(query_tokens, wk[...]).astype(BF)
        query_values = dot(query_tokens, wv[...]).astype(BF)
        for p in range(pairs):
            k_buf[p, pl.ds(2 * half, q_rows)] = query_keys
            v_buf[p, pl.ds(2 * half, q_rows)] = query_values

    lane = lax.broadcasted_iota(jnp.int32, (1, 2 * half + q_rows), 1)
    local = lax.broadcasted_iota(jnp.int32, (block, 1), 0)

    def pair_row(p):
        chosen = pair_list[p, 0]
        sources = [pair_list[p, 1], pair_list[p, 2]]
        lengths = [doc_len[s * docs + jnp.maximum(route[s, me], 0)] for s in sources]
        own = jnp.concatenate([arrived[s].astype(F32) for s in sources], 0)
        tokens[p] = own

        def gather(stage, values):
            def part(n):
                return gathered.at[stage, p, pl.ds(pl.multiple_of(n * block, block), block)]

            slot = stage * pairs + p
            gathered[stage, p, pl.ds(pl.multiple_of(z * block, block), block)] = values
            first, second = gather_copies(part, slot)
            for copy in first:
                start(copy)
            yield
            first[0].wait_recv()
            first[1].wait_recv()
            for copy in second:
                start(copy)
            yield
            for copy in first[2:] + second:
                copy.wait_recv()
            other = start(
                send(
                    gathered.at[stage, p, pl.ds(0, half)],
                    gathered.at[stage, p, pl.ds(half, half)],
                    core_send.at[slot],
                    core_recv.at[slot],
                    partner,
                )
            )
            yield
            other.wait_recv()

        def core_copy(stage):
            slot = 2 * pairs + stage * pairs + p
            return send(
                half_out.at[stage, p],
                half_in.at[stage, p],
                core_send.at[slot],
                core_recv.at[slot],
                partner,
            )

        def reduce(stage, other):
            slot = stage * pairs + p
            other.wait_recv()

            def chip_rows(origin):
                return pl.ds(pl.multiple_of(level(origin) * block, block), block)

            def chip_sum(origin):
                rows_of = chip_rows(origin)
                return mine[p, rows_of] + half_in[stage, p, rows_of].astype(F32)

            def one(n, origin, k, src=None):
                part = ring_out.at[stage, p, chip_rows(origin)] if src is None else src
                return start(
                    send(
                        part,
                        ring_in.at[stage, p, n],
                        ring_send.at[slot, n],
                        ring_recv.at[slot, n],
                        peer(k),
                    )
                )

            for origin in (4, 3, -3):
                ring_out[stage, p, chip_rows(origin)] = chip_sum(origin).astype(BF)
            first = [one(1, 4, 2), one(0, 3, 1), one(2, -3, -1)]
            for origin in (1, -1):
                ring_out[stage, p, chip_rows(origin)] = chip_sum(origin).astype(BF)
            near = [one(3, 1, 1), one(4, -1, -1)]
            for origin in (0, 2, -2):
                mine[p, chip_rows(origin)] = chip_sum(origin)
            yield
            first[2].wait_recv()
            ring_sum[stage, p, 1] = (
                mine[p, chip_rows(-2)] + ring_in[stage, p, 2].astype(F32)
            ).astype(BF)
            first[1].wait_recv()
            partial = mine[p, chip_rows(2)] + ring_in[stage, p, 0].astype(F32)
            first[0].wait_recv()
            ring_sum[stage, p, 0] = (partial + ring_in[stage, p, 1].astype(F32)).astype(BF)
            far = [
                one(5, 2, 2, ring_sum.at[stage, p, 0]),
                one(6, -2, -2, ring_sum.at[stage, p, 1]),
            ]
            yield
            for copy in near + far:
                copy.wait_recv()
            total = mine[p, chip_rows(0)]
            for n in range(3, 7):
                total = total + ring_in[stage, p, n].astype(F32)
            return total

        yield from gather(0, rms_norm(own, gain).astype(BF))

        if p == 0:
            weights[2].wait()
        x = gathered[0, p]
        q_buf[p] = dot(x, wq[...]).astype(BF)
        k_buf[p, pl.ds(0, 2 * half)] = dot(x, wk[...]).astype(BF)
        v_buf[p, pl.ds(0, 2 * half)] = dot(x, wv[...]).astype(BF)
        yield
        ring_place = (lane % half) // block
        held_by = jnp.where(lane < half, core, 1 - core)
        position = (ring_place * 2 + held_by) * rows + lane % rows
        limit = jnp.where(lane % block < rows, lengths[0], lengths[1])
        doc_ok = jnp.where(position < limit, 1.0, 0.0)
        query_ok = jnp.where((lane % query_rows) // query_part_rows == chosen, 1.0, 0.0)
        key_ok = jnp.where(lane < 2 * half, doc_ok, query_ok)
        for h in range(heads):
            cols = pl.ds(h * HEAD, HEAD)
            scores = lax.dot_general(
                q_buf[p, :, cols],
                k_buf[p, :, cols],
                (((1,), (1,)), ((), ())),
                preferred_element_type=F32,
            ) * (1.0 / math.sqrt(HEAD))
            scores = jnp.where(key_ok > 0.5, scores, -1e30)
            expo = jnp.exp(scores - jnp.max(scores, -1, keepdims=True))
            probs = (expo * (1.0 / jnp.sum(expo, -1, keepdims=True))).astype(BF)
            context[p, :, cols] = dot(probs, v_buf[p, :, cols]).astype(BF)
        if p == 0:
            weights[3].wait()
        half_out[0, p] = dot(context[p, pl.ds(half, half)], wo[...]).astype(BF)
        other = start(core_copy(0))
        mine[p] = dot(context[p, pl.ds(0, half)], wo[...])
        yield
        hidden = tokens[p] + (yield from reduce(0, other))
        tokens[p] = hidden
        yield from gather(1, rms_norm(hidden, ffn_gain[...]).astype(BF))

        if p == 0:
            weights[4].wait()

        def up(n, _):
            cols = pl.ds(pl.multiple_of(n * 512, 512), 512)
            units[:, cols] = jnp.maximum(dot(gathered[1, p], wi[:, cols]), 0.0).astype(BF)
            return 0

        lax.fori_loop(0, units.shape[1] // 512, up, 0)
        yield
        if p == 0:
            weights[5].wait()

        def down(n, _):
            cols = pl.ds(pl.multiple_of(n * 256, 256), 256)
            term = dot(units[...], wd[:, cols])
            mine[p, :, cols] = term[:half]
            half_out[1, p, :, cols] = term[half:].astype(BF)
            return 0

        lax.fori_loop(0, width // 256, down, 0)
        other = start(core_copy(1))
        yield
        layer_out = tokens[p] + (yield from reduce(1, other))
        position = place * rows + local % rows
        limit = jnp.where(local < rows, lengths[0], lengths[1])
        layer_out = jnp.where(position < limit, layer_out, 0.0)
        results[2 * p] = layer_out[:rows].astype(BF)
        results[2 * p + 1] = layer_out[rows:].astype(BF)

    programs = [pair_row(p) for p in range(pairs)] + [query_program()]
    for p in ORDER:
        next(programs[p], None)

    for o in range(owners):
        back[o] = results[roles[o]]
    returned[me] = back[me]
    earlier = len(started)
    home = [start(pair_copy(d, back, returned, 1)) for d in range(1, owners)]
    for copy in started[:earlier]:
        copy.wait_send()
    for copy in home:
        copy.wait_recv()
    for k in range(docs):
        total = jnp.zeros((rows, width), F32)
        for o in range(owners):
            total = total + jnp.where(route[me, o] == k, returned[o].astype(F32), 0.0)
        out[k] = total.astype(BF)
    for copy in home:
        copy.wait_send()


def solution(mesh):
    owners = mesh.shape["pair"]
    ring = mesh.shape["tensor"] // 2
    spread = P("pair", "tensor", None)

    def local(
        queries, documents, doc_len, route, pair_list, attn_gain, wq, wk, wv, wo, ffn_gain, wi, wd
    ):
        pairs = pair_list.shape[0]
        docs, rows, width = documents.shape
        query_rows = queries.shape[0] * queries.shape[1]
        head_width, unit_count = wq.shape[1], wi.shape[1]
        block = 2 * rows
        half = ring * block
        keys = 2 * half + 2 * ring * query_rows
        vmem = pl.BlockSpec(memory_space=pltpu.VMEM)
        hbm = pl.BlockSpec(memory_space=pl.ANY)
        dma = pltpu.SemaphoreType.DMA
        return pl.pallas_call(
            functools.partial(layer_kernel, owners, ring),
            out_shape=pltpu.VMEM((docs, rows, width), BF),
            in_specs=[hbm] * 13,
            out_specs=vmem,
            scratch_shapes=[
                pltpu.SMEM(doc_len.shape, jnp.int32),
                pltpu.SMEM(route.shape, jnp.int32),
                pltpu.SMEM(pair_list.shape, jnp.int32),
                pltpu.VMEM(queries.shape, BF),
                pltpu.VMEM(documents.shape, BF),
                pltpu.VMEM((1, width), F32),
                pltpu.VMEM((1, width), F32),
                pltpu.VMEM(wq.shape, BF),
                pltpu.VMEM(wk.shape, BF),
                pltpu.VMEM(wv.shape, BF),
                pltpu.VMEM(wo.shape, BF),
                pltpu.VMEM(wi.shape, BF),
                pltpu.VMEM(wd.shape, BF),
                pltpu.VMEM((owners, rows, width), BF),
                pltpu.VMEM((owners, rows, width), BF),
                pltpu.VMEM((2 * ring, query_rows, width), BF),
                pltpu.VMEM((2, pairs, 2 * half, width), BF),
                pltpu.VMEM((pairs, block, width), F32),
                pltpu.VMEM((pairs, 2 * half, head_width), BF),
                pltpu.VMEM((pairs, keys, head_width), BF),
                pltpu.VMEM((pairs, keys, head_width), BF),
                pltpu.VMEM((pairs, 2 * half, head_width), BF),
                pltpu.VMEM((2 * half, unit_count), BF),
                pltpu.VMEM((pairs, half, width), F32),
                pltpu.VMEM((2, pairs, half, width), BF),
                pltpu.VMEM((2, pairs, half, width), BF),
                pltpu.VMEM((2, pairs, half, width), BF),
                pltpu.VMEM((2, pairs, 7, block, width), BF),
                pltpu.VMEM((2, pairs, 2, block, width), BF),
                pltpu.VMEM((2 * pairs + 1, rows, width), BF),
                pltpu.VMEM((owners, rows, width), BF),
                pltpu.VMEM((owners, rows, width), BF),
                dma((7,)),
                dma((6,)),
                dma((2, owners)),
                dma((2, owners)),
                dma((2 * pairs + 1, 7)),
                dma((2 * pairs + 1, 7)),
                dma((4 * pairs + 1,)),
                dma((4 * pairs + 1,)),
                dma((2 * pairs, 7)),
                dma((2 * pairs, 7)),
            ],
            compiler_params=pltpu.CompilerParams(
                collective_id=0, has_side_effects=True, vmem_limit_bytes=60 * 1024 * 1024
            ),
        )(
            doc_len,
            route,
            pair_list,
            queries,
            documents,
            attn_gain.reshape(1, width),
            ffn_gain.reshape(1, width),
            wq,
            wk,
            wv,
            wo,
            wi,
            wd,
        )

    placed = (
        spread,
        spread,
        P(),
        P(),
        P("pair", None),
        P(),
        P(None, "tensor"),
        P(None, "tensor"),
        P(None, "tensor"),
        P("tensor", None),
        P(),
        P(None, "tensor"),
        P("tensor", None),
    )
    return jax.shard_map(local, mesh=mesh, in_specs=placed, out_specs=spread, check_vma=False)
```
